32 devices in a mesh: head: 4 (over y, core), ctx: 8 (over z, x).
Axes of the slice: x: 2, y: 2, z: 4, core: 2. Of those that a mesh axis runs over, the one named last changes fastest.
Arguments:
- queries: bfloat16 [16384, 4096], P('ctx', 'head'), may hold values from -6 to 6
- keys: bfloat16 [16384, 4096], P('ctx', 'head'), may hold values from -6 to 6
- values: bfloat16 [16384, 4096], P('ctx', 'head'), may hold values from -23 to 23
- level_table: float32 [4, 7], replicated, may hold values from 0.3 to 3
- head_table: int32 [32], replicated, may hold values from 0 to 3
- gain: float32 [4096], P('head'), may hold values from 0.5 to 1.5
Outputs:
- attended: bfloat16 [16384, 4096], P('ctx', 'head')
The draws below stay inside these ranges and needn't reach their ends.
All inputs are finite; a program needn't handle non-finite values.
Results may differ from the reference program's by a relative error of at most 0.0043.
Values sent between devices are 32-bit elements; how exact they have to be, the bound alone decides.
No kernel may reach another device: no remote copies, remote signals or barrier semaphores. Data moves between devices by JAX's collectives and lax.ppermute only.
A program may use at most 192 MiB of HBM per device.

```python
import math
import jax
import jax.numpy as jnp
from jax import lax

HEADS = 32
HEAD_DIM = 128
LEAF = 256
PROFILES = 4
SEG = 2048
TOKENS = 16384
D = 4096
LOCAL_BITS = 3
CTX_BITS = 3
LEVELS = 7
N_CTX = 8


def draw_values(key, part):
    first_key, second_key = jax.random.split(key, 2)
    head_ramp = jnp.arange(HEADS, dtype=jnp.float32) / max(HEADS - 1, 1)
    head_scale = jnp.exp(jnp.log(3.0) * head_ramp) * jax.random.uniform(second_key, (HEADS,), jnp.float32, 0.8, 1.25)
    columns = jnp.repeat(head_scale, HEAD_DIM)
    base = jnp.clip(jax.random.normal(first_key, (TOKENS, D), jnp.float32), -6.0, 6.0)
    return (base * columns[None, :]).astype(jnp.bfloat16)


def with_ends(array, rng, low, top_value):
    longest = array.shape.index(max(array.shape))
    spots = []
    for shift in (0, 1):
        where = [jax.random.randint(jax.random.fold_in(rng, axis), (), 0, length) for axis, length in enumerate(array.shape)]
        where[longest] = (where[longest] + shift) % array.shape[longest]
        spots.append(tuple(where))
    return array.at[spots[0]].set(low).at[spots[1]].set(top_value)


def level_of(stream_key, dims, cuts, low, top_value):
    level = 1.0
    for axis_at, blocks in cuts:
        draws = jax.random.uniform(jax.random.fold_in(jax.random.fold_in(stream_key, 6), axis_at), (blocks,), jnp.float32, low / len(cuts), top_value / len(cuts))
        level = level * jnp.repeat(jnp.exp(draws), dims[axis_at] // blocks).reshape((-1,) + (1,) * (len(dims) - 1 - axis_at))
    return level


def scatter_about(own_key, extent, scale, most, shards=(), kind=jnp.bfloat16):
    loudness = level_of(own_key, extent, shards, -0.22, 0.18) if shards else 1.0
    array = jax.random.normal(own_key, extent, jnp.float32) * scale * loudness
    return jnp.minimum(jnp.maximum(array, -most), most).astype(kind)


def setup_inputs(seed: int = 0) -> dict:
    arg_keys = jax.random.split(jax.random.key(seed), 7)
    queries = scatter_about(arg_keys[0], (TOKENS, D), 1.0, 6.0, ((0, 8), (1, 4)))
    keys = scatter_about(arg_keys[1], (TOKENS, D), 1.0, 6.0, ((0, 8), (1, 4)))
    values = draw_values(jax.random.fold_in(arg_keys[6], 71), 0)
    level_table = jnp.clip(jnp.exp(jax.random.uniform(arg_keys[3], (PROFILES, LEVELS), jnp.float32, math.log(0.3), math.log(3.0))), 0.3, 3.0)
    head_table = with_ends(jax.random.randint(arg_keys[4], (HEADS,), 0, PROFILES), jax.random.fold_in(arg_keys[4], 1), 0, PROFILES - 1).astype(jnp.int32)
    gain = jnp.clip(1.0 + 0.1 * jax.random.normal(arg_keys[5], (D,), jnp.float32), 0.5, 1.5)
    return dict(queries=queries, keys=keys, values=values, level_table=level_table, head_table=head_table, gain=gain)


epsilon = 1e-06

def level_scales(level_count):
    level_ids = jnp.arange(level_count, dtype=jnp.int32)
    bucket_sizes = jnp.exp2(jnp.maximum(level_ids - 1, 0).astype(jnp.float32)) * jnp.float32(LEAF)
    return 1.0 / jnp.sqrt(bucket_sizes)

def tile_levels(query_pos, key_pos, local_bits):
    distance = jnp.bitwise_xor((query_pos // LEAF)[:, None], (key_pos // LEAF)[None, :])
    level_ids = jnp.zeros(distance.shape, jnp.int32)
    for level_bit in range(local_bits):
        level_ids = level_ids + (distance >= 1 << level_bit).astype(jnp.int32)
    return level_ids

def tile_weights(query_pos, key_pos, effective, local_bits):
    level_ids = tile_levels(query_pos, key_pos, local_bits)
    weight = jnp.zeros((effective.shape[0],) + level_ids.shape, effective.dtype)
    for level_num in range(local_bits + 1):
        member = jnp.where(level_ids == level_num, 1.0, 0.0).astype(effective.dtype)
        weight = weight + member[None] * effective[:, level_num, None, None]
    causal = key_pos[None, :] <= query_pos[:, None]
    return jnp.where(causal[None], weight, 0.0)

def reference(queries, keys, values, level_table, head_table, gain):
    selector = (head_table[:, None] == jnp.arange(PROFILES, dtype=jnp.int32)[None, :]).astype(jnp.float32)
    chosen = jnp.dot(selector, level_table, precision=lax.Precision.HIGHEST)
    effective = chosen * level_scales(LEVELS)[None, :]
    query_all = queries.reshape(N_CTX, SEG, HEADS, HEAD_DIM)
    key_all = keys.reshape(N_CTX, SEG, HEADS, HEAD_DIM)
    value_all = values.reshape(N_CTX, SEG, HEADS, HEAD_DIM)

    def segment_state(operand):
        return jnp.einsum('thd,the->hde', operand[0].astype(jnp.float32), operand[1].astype(jnp.float32))
    states = lax.map(segment_state, (key_all, value_all))
    segment_ids = jnp.arange(N_CTX, dtype=jnp.int32)
    distant = jnp.zeros_like(states)
    for level_bit in range(CTX_BITS):
        grouped = states.reshape(N_CTX >> level_bit + 1, 2, 1 << level_bit, HEADS, HEAD_DIM, HEAD_DIM)
        sibling_sums = lax.optimization_barrier(jnp.sum(grouped[:, 0], axis=1))
        siblings = jnp.repeat(sibling_sums, 2 << level_bit, axis=0)
        member = (segment_ids >> level_bit & 1).astype(jnp.float32)
        factor = member[:, None] * effective[None, :, LOCAL_BITS + 1 + level_bit]
        distant = distant + factor[:, :, None, None] * siblings
    key_pos = jnp.arange(SEG, dtype=jnp.int32)

    def segment_out(operand):
        query_seg, key_seg, value_seg, distant_seg = operand

        def head_out(inner):
            query_head, key_head, value_head, eff_row = inner
            scores = jnp.dot(query_head, key_head.T, preferred_element_type=jnp.float32)
            weight = tile_weights(key_pos, key_pos, eff_row[None, :], LOCAL_BITS)[0]
            rounded = (scores * weight).astype(jnp.bfloat16)
            return jnp.dot(rounded, value_head, preferred_element_type=jnp.float32)
        nearby = lax.map(head_out, (jnp.swapaxes(query_seg, 0, 1), jnp.swapaxes(key_seg, 0, 1), jnp.swapaxes(value_seg, 0, 1), effective))
        nearby = jnp.swapaxes(nearby, 0, 1)
        remote = jnp.einsum('thd,hde->the', query_seg.astype(jnp.float32), distant_seg, precision=lax.Precision.HIGHEST)
        return nearby + remote
    combined = lax.map(segment_out, (query_all, key_all, value_all, distant)).reshape(TOKENS, D)
    squares = lax.optimization_barrier(jnp.sum(combined * combined, axis=1))
    inverse = lax.rsqrt(squares / D + epsilon)
    return (combined * inverse[:, None] * gain[None, :]).astype(jnp.bfloat16)
```

```python
import functools

import jax
import jax.numpy as jnp
from jax import lax
from jax.experimental import pallas as pl
from jax.experimental.pallas import tpu as pltpu
from jax.sharding import PartitionSpec as P

HEAD_DIM = 128
LEAF = 256
CHUNKS = 4

epsilon = 1e-06
f32 = jnp.float32
bf16 = jnp.bfloat16


def level_scales(level_count):
    level_ids = jnp.arange(level_count, dtype=jnp.int32)
    bucket_sizes = jnp.exp2(jnp.maximum(level_ids - 1, 0).astype(f32)) * f32(LEAF)
    return 1.0 / jnp.sqrt(bucket_sizes)


def split_rows(matrix):
    high = matrix.astype(bf16)
    low = (matrix - high.astype(f32)).astype(bf16)
    return jnp.concatenate([high, low], axis=0)


def doubled(rows):
    return jnp.concatenate([rows, rows], axis=1)


def dot(left, right):
    return jnp.dot(left, right, preferred_element_type=f32)


def dot_tokens(left, right):
    return lax.dot_general(left, right, (((0,), (0,)), ((), ())), preferred_element_type=f32)


def dot_features(left, right):
    return lax.dot_general(left, right, (((1,), (1,)), ((), ())), preferred_element_type=f32)


def state_kernel(key_ref, value_ref, state_ref):
    state_ref[0] = dot_tokens(key_ref[...], value_ref[...])


def local_kernel(first, weight_ref, query_ref, key_ref, value_ref, out_ref):
    head = first + pl.program_id(0)
    leaves = query_ref.shape[0] // LEAF
    bits = leaves.bit_length() - 1
    row = lax.broadcasted_iota(jnp.int32, (LEAF, LEAF), 0)
    column = lax.broadcasted_iota(jnp.int32, (LEAF, LEAF), 1)
    own_weight = jnp.where(column <= row, weight_ref[head, 0], 0.0)
    waiting = {}
    for leaf in range(leaves):
        rows = pl.ds(leaf * LEAF, LEAF)
        query, key, value = query_ref[rows, :], key_ref[rows, :], value_ref[rows, :]
        rounded = (dot_features(query, key) * own_weight).astype(bf16)
        near = dot(rounded, value)
        siblings = None
        for bit in range(bits):
            if leaf >> bit & 1:
                term = weight_ref[head, 1 + bit] * waiting[bit]
                siblings = term if siblings is None else siblings + term
        if siblings is not None:
            near = near + dot(doubled(query), split_rows(siblings))
        out_ref[rows, :] = near
        if leaf + 1 < leaves:
            block = dot_tokens(key, value)
            bit = 0
            while leaf >> bit & 1:
                block = waiting.pop(bit) + block
                bit += 1
            waiting[bit] = block


def distant_kernel(first, parts, has_sum, *refs):
    coefficient_ref, query_ref, near_ref = refs[:3]
    part_refs = refs[3 : 3 + parts]
    sum_ref = refs[3 + parts] if has_sum else None
    combined_ref, squares_ref, total_ref = refs[-3:]
    step = pl.program_id(0)
    rows = query_ref.shape[0]
    distant = coefficient_ref[first + step, 0] * part_refs[0][0]
    for num in range(1, parts):
        distant = distant + coefficient_ref[first + step, num] * part_refs[num][0]
    terms = split_rows(distant)
    last = step == pl.num_programs(0) - 1
    for start in range(0, rows, LEAF):
        here = pl.ds(start, LEAF)
        combined = near_ref[here, :] + dot(doubled(query_ref[here, :]), terms)
        combined_ref[here, :] = combined
        squares = combined * combined

        @pl.when(step == 0)
        def _():
            total_ref[here, :] = squares

        @pl.when(step > 0)
        def _():
            total_ref[here, :] += squares

    @pl.when(last)
    def _():
        for start in range(0, rows, HEAD_DIM):
            flipped = total_ref[pl.ds(start, HEAD_DIM), :].T
            sums = jnp.sum(flipped, axis=0, keepdims=True)
            if has_sum:
                sums = sums + sum_ref[:, pl.ds(start, HEAD_DIM)]
            squares_ref[:, pl.ds(start, HEAD_DIM)] = sums


def finish_kernel(chunks, others, width, *refs):
    chunk_refs = refs[:chunks]
    sum_refs = refs[chunks : chunks + 1 + others]
    gain_ref, out_ref = refs[-2:]
    total = sum_refs[0][...]
    for ref in sum_refs[1:]:
        total = total + ref[...]
    inverse = lax.rsqrt(total / width + epsilon)
    column = 0
    for start in range(0, out_ref.shape[0], HEAD_DIM):
        spread = jnp.broadcast_to(inverse[:, start : start + HEAD_DIM], (HEAD_DIM, HEAD_DIM)).T
        here = pl.ds(start, HEAD_DIM)
        column = 0
        for ref in chunk_refs:
            for part in range(0, ref.shape[1], HEAD_DIM):
                gain = gain_ref[:, pl.ds(column, HEAD_DIM)]
                out_ref[here, pl.ds(column, HEAD_DIM)] = (
                    ref[here, pl.ds(part, HEAD_DIM)] * spread * gain
                ).astype(bf16)
                column += HEAD_DIM


def params(mib):
    return pltpu.CompilerParams(vmem_limit_bytes=mib * 2**20)


SMEM = pl.BlockSpec(memory_space=pltpu.SMEM)


def states_of(keys, values, first, count):
    rows = keys.shape[0]
    block = pl.BlockSpec((rows, HEAD_DIM), lambda h: (0, first + h))
    return pl.pallas_call(
        state_kernel,
        name="states",
        grid=(count,),
        in_specs=[block, block],
        out_specs=pl.BlockSpec((1, HEAD_DIM, HEAD_DIM), lambda h: (h, 0, 0)),
        out_shape=jax.ShapeDtypeStruct((count, HEAD_DIM, HEAD_DIM), f32),
        compiler_params=params(8),
        cost_estimate=pl.CostEstimate(
            flops=2 * count * rows * HEAD_DIM**2,
            bytes_accessed=4 * count * rows * HEAD_DIM,
            transcendentals=0,
        ),
    )(keys, values)


def local_of(effective, queries, keys, values, first, count):
    rows = keys.shape[0]
    block = pl.BlockSpec((rows, HEAD_DIM), lambda h: (0, first + h))
    return pl.pallas_call(
        functools.partial(local_kernel, first),
        name="local",
        grid=(count,),
        in_specs=[SMEM, block, block, block],
        out_specs=pl.BlockSpec((rows, HEAD_DIM), lambda h: (0, h)),
        out_shape=jax.ShapeDtypeStruct((rows, count * HEAD_DIM), f32),
        compiler_params=params(12),
        cost_estimate=pl.CostEstimate(
            flops=8 * count * rows * LEAF * HEAD_DIM,
            bytes_accessed=10 * count * rows * HEAD_DIM,
            transcendentals=0,
        ),
    )(effective, queries, keys, values)


def distant_of(coefficients, queries, near, parts, sums, first):
    rows = queries.shape[0]
    count = parts[0].shape[0]
    matrix = pl.BlockSpec((1, HEAD_DIM, HEAD_DIM), lambda h: (h, 0, 0))
    near_block = pl.BlockSpec((rows, HEAD_DIM), lambda h: (0, h))
    line = pl.BlockSpec((1, rows), lambda h: (0, 0))
    extra = [] if sums is None else [sums]
    return pl.pallas_call(
        functools.partial(distant_kernel, first, len(parts), bool(extra)),
        name="distant",
        grid=(count,),
        in_specs=[SMEM, pl.BlockSpec((rows, HEAD_DIM), lambda h: (0, first + h)), near_block]
        + [matrix] * len(parts)
        + [line] * len(extra),
        out_specs=[near_block, line],
        out_shape=[
            jax.ShapeDtypeStruct((rows, count * HEAD_DIM), f32),
            jax.ShapeDtypeStruct((1, rows), f32),
        ],
        scratch_shapes=[pltpu.VMEM((rows, HEAD_DIM), f32)],
        input_output_aliases={2: 0},
        compiler_params=params(12),
        cost_estimate=pl.CostEstimate(
            flops=4 * count * rows * HEAD_DIM**2,
            bytes_accessed=10 * count * rows * HEAD_DIM,
            transcendentals=0,
        ),
    )(coefficients, queries, near, *parts, *extra)


def finish_of(pieces, sums, gain, width):
    rows = pieces[0].shape[0]
    columns = gain.shape[1]
    block_rows = min(512, rows)
    line = pl.BlockSpec((1, block_rows), lambda i: (0, i))
    return pl.pallas_call(
        functools.partial(finish_kernel, len(pieces), len(sums) - 1, width),
        name="finish",
        grid=(rows // block_rows,),
        in_specs=[pl.BlockSpec((block_rows, p.shape[1]), lambda i: (i, 0)) for p in pieces]
        + [line] * len(sums)
        + [pl.BlockSpec((1, columns), lambda i: (0, 0))],
        out_specs=pl.BlockSpec((block_rows, columns), lambda i: (i, 0)),
        out_shape=jax.ShapeDtypeStruct((rows, columns), bf16),
        compiler_params=params(16),
        cost_estimate=pl.CostEstimate(
            flops=2 * rows * columns, bytes_accessed=6 * rows * columns, transcendentals=rows
        ),
    )(*pieces, *sums, gain)


def hop(array, pairs):
    return lax.ppermute(array, "ctx", pairs)


def tree_parts(state, bits):
    size = 1 << bits
    total, parts = state, []
    for bit in range(bits):
        got = hop(total, [(i, i ^ 1 << bit) for i in range(size)])
        parts.append(got)
        if bit + 1 < bits:
            total = total + got
    return parts


PAIRS = [(i, i ^ 1) for i in range(8)]
HOPS = [[(2 * z + x, 2 * z + 2 + x) for x in (0, 1)] for z in range(3)]


def pair_first_parts(state, weights):
    swapped = hop(state, PAIRS)
    pair = state + swapped
    first = hop(pair, HOPS[0])
    second = hop(pair + first, HOPS[1])
    third = hop(weights[1] * pair + weights[2] * second, HOPS[2])
    return [swapped, first, second, third]


def pair_last_parts(state, weights, even):
    first = hop(state, HOPS[0])
    second = hop(state + first, HOPS[1])
    third = hop(weights[1] * state + weights[2] * second, HOPS[2])
    column = weights[1] * first + weights[2] * second + third
    swapped = hop(column + even * weights[0] * state, PAIRS)
    return [swapped, first, second, third]


def body(queries, keys, values, level_table, head_table, gain, *, width):
    rows = queries.shape[0]
    heads = queries.shape[1] // HEAD_DIM
    local_bits = (rows // LEAF).bit_length() - 1
    ctx_size, head_size = lax.axis_size("ctx"), lax.axis_size("head")
    ctx_bits = ctx_size.bit_length() - 1
    segment = lax.axis_index("ctx")
    table = lax.dynamic_slice_in_dim(head_table, lax.axis_index("head") * heads, heads, 0)
    mine = jnp.zeros((heads, level_table.shape[1]), f32)
    for profile in range(level_table.shape[0]):
        mine = jnp.where(table[:, None] == profile, level_table[profile][None, :], mine)
    effective = mine * level_scales(level_table.shape[1])[None, :]
    far = effective[:, local_bits + 1 :]
    bit_on = (segment >> jnp.arange(ctx_bits, dtype=jnp.int32) & 1).astype(f32)
    chunks = CHUNKS if heads % CHUNKS == 0 else 1
    count = heads // chunks
    even = 1.0 - bit_on[0]

    parts, coefficients = [], []
    for chunk in range(chunks):
        first = chunk * count
        state = states_of(keys, values, first, count)
        if ctx_bits == 3:
            weights = [far[first : first + count, b][:, None, None] for b in range(3)]
            one = jnp.ones((heads,), f32)
            if chunk % 2 == 0:
                parts.append(pair_first_parts(state, weights))
                lead = far[:, 0] * bit_on[0]
            else:
                parts.append(pair_last_parts(state, weights, even))
                lead = one
            coefficients.append(jnp.stack([lead, far[:, 1], far[:, 2], one], axis=1))
        else:
            parts.append(tree_parts(state, ctx_bits))
            coefficients.append(far * bit_on[None, :])
    near = [
        local_of(effective, queries, keys, values, chunk * count, count) for chunk in range(chunks)
    ]
    sums, pieces = None, []
    for chunk in range(chunks):
        piece, sums = distant_of(
            coefficients[chunk], queries, near[chunk], parts[chunk], sums, chunk * count
        )
        pieces.append(piece)
    everyone = [sums]
    for shift in range(1, head_size):
        everyone.append(lax.ppermute(sums, "head", [(i, i ^ shift) for i in range(head_size)]))
    return finish_of(pieces, everyone, gain[None, :], width)


def solution(mesh):
    def run(queries, *rest):
        return jax.shard_map(
            functools.partial(body, width=queries.shape[1]),
            mesh=mesh,
            in_specs=(P("ctx", "head"), P("ctx", "head"), P("ctx", "head"), P(), P(), P("head")),
            out_specs=P("ctx", "head"),
            check_vma=False,
        )(queries, *rest)

    return run
```
